256 devices in a mesh: col: 8 (over z_lo, core), dp: 32 (over z_hi, y, x).
Axes of the slice: x: 4, y: 4, z: 8 (z_hi: 2, z_lo: 4; z = z_hi * 4 + z_lo), core: 2. Of those that a mesh axis runs over, the one named last changes fastest.
Arguments:
- acts: bfloat16 [12288, 5120], P('dp', 'col'), may hold values from -6 to 6
- out_grad: bfloat16 [12288, 8192], P('dp', 'col'), may hold values from -6 to 6
- projection: bfloat16 [5120, 256], replicated, may hold values from -0.078125 to 0.078125
- weight: bfloat16 [5120, 8192], P('dp', 'col'), may hold values from -0.078125 to 0.078125
- m_codes: int32 [256, 8192], P('dp', 'col'), may hold values from -127 to 127
- m_exps: int32 [256, 256], P('dp', 'col'), may hold values from -16 to -9
- v_codes: int32 [256, 8192], P('dp', 'col'), may hold values from 1 to 127
- v_exps: int32 [256, 256], P('dp', 'col'), may hold values from -24 to -18
- next_acts: bfloat16 [12288, 5120], P('dp', 'col'), may hold values from -6 to 6
Outputs:
- next_out: bfloat16 [12288, 8192], P('dp', 'col')
- new_weight: bfloat16 [5120, 8192], P('dp', 'col')
- update: float32 [256, 8192], P('dp', 'col')
The draws below stay inside these ranges and needn't reach their ends.
Inputs may be any that keep to these rules, and one draw needn't show every extreme that they name: `v_codes`: second moment mantissas are positive.
All inputs are finite; a program needn't handle non-finite values.
Results may differ from the reference program's by a relative error of at most 0.0051.
Values may be sent and summed in bfloat16 or wider, within the bound.
No kernel may reach another device: no remote copies, remote signals or barrier semaphores. Data moves between devices by JAX's collectives and lax.ppermute only.
A program may use at most 128 MiB of HBM per device.

```python
import jax
import jax.numpy as jnp
from jax import lax

D = 5120
F = 8192
R = 256
BLOCK = 32
TOKENS = 12288


def with_ends(values, rng, least, top_value):
    extent = values.shape
    index_at = [jax.random.randint(jax.random.fold_in(rng, axis), (), 0, extent[axis]) for axis in range(len(extent))]
    values = values.at[tuple(index_at)].set(least)
    longest = extent.index(max(extent))
    index_at[longest] = (index_at[longest] + 1) % extent[longest]
    return values.at[tuple(index_at)].set(top_value)


def block_scale(own_key, shape, pieces, low, high):
    def one(axis_at, shards_of):
        heights = jax.random.uniform(jax.random.fold_in(jax.random.fold_in(own_key, 6), axis_at), (shards_of,), jnp.float32, low / len(pieces), high / len(pieces))
        return jnp.repeat(jnp.exp(heights), shape[axis_at] // shards_of).reshape((-1,) + (1,) * (len(shape) - axis_at - 1))

    loudness = one(*pieces[0])
    for cut in pieces[1:]:
        loudness = loudness * one(*cut)
    return loudness


def bell_draw(rng, extent, width, bound, shards=(), kind=jnp.bfloat16):
    factor_of = block_scale(rng, extent, shards, -0.22, 0.18) if shards else 1.0
    entries = jax.random.normal(rng, extent, jnp.float32) * width * factor_of
    return jnp.minimum(jnp.maximum(entries, -bound), bound).astype(kind)


def setup_inputs(seed: int = 0) -> dict:
    splits = jax.random.split(jax.random.key(seed), 10)
    acts = bell_draw(splits[0], (TOKENS, D), 1.0, 6.0, ((0, 32), (1, 8)))
    out_grad = bell_draw(splits[1], (TOKENS, F), 1.0, 6.0, ((0, 32), (1, 8)))
    projection = bell_draw(splits[2], (D, R), D ** -0.5, 0.078125)
    weight = bell_draw(splits[3], (D, F), D ** -0.5, 0.078125, ((0, 32), (1, 8)))
    m_codes = with_ends(jax.random.randint(splits[4], (R, F), -127, 128), jax.random.fold_in(splits[4], 1), -127, 127).astype(jnp.int32)
    m_exps = with_ends(jax.random.randint(splits[5], (R, F // BLOCK), -16, -8), jax.random.fold_in(splits[5], 1), -16, (-8) - 1).astype(jnp.int32)
    v_codes = with_ends(jax.random.randint(splits[6], (R, F), 1, 128), jax.random.fold_in(splits[6], 1), 1, 127).astype(jnp.int32)
    v_exps = with_ends(jax.random.randint(splits[7], (R, F // BLOCK), -24, -17), jax.random.fold_in(splits[7], 1), -24, (-17) - 1).astype(jnp.int32)
    next_acts = bell_draw(splits[8], (TOKENS, D), 1.0, 6.0, ((0, 32), (1, 8)))
    return {"acts": acts, "out_grad": out_grad, "projection": projection, "weight": weight, "m_codes": m_codes, "m_exps": m_exps, "v_codes": v_codes, "v_exps": v_exps, "next_acts": next_acts}


learn_rate = 0.02
beta_one = 0.9
beta_two = 0.999
epsilon = 1e-08
correct_first = 0.9999734386011124
correct_second = 0.0952078528862904

def decode(codes, exps):
    scale = jnp.exp2(exps.astype(jnp.float32))
    rows = codes.shape[0]
    values = (codes.astype(jnp.float32) / 128.0).reshape(rows, exps.shape[1], codes.shape[1] // exps.shape[1])
    return (values * scale[:, :, None]).reshape(rows, codes.shape[1])

def reference(acts, out_grad, projection, weight, m_codes, m_exps, v_codes, v_exps, next_acts):
    lowrank = jnp.dot(acts, projection, preferred_element_type=jnp.float32).astype(jnp.bfloat16)
    grad = lax.dot_general(lowrank, out_grad, (((0,), (0,)), ((), ())), preferred_element_type=jnp.float32) / TOKENS
    m_old = decode(m_codes, m_exps)
    v_old = decode(v_codes, v_exps)
    first = beta_one * m_old + (1.0 - beta_one) * grad
    second = beta_two * v_old + (1.0 - beta_two) * grad * grad
    update = first / correct_first / (jnp.sqrt(second / correct_second) + epsilon)
    direction = update.astype(jnp.bfloat16)
    delta = jnp.dot(projection, direction, preferred_element_type=jnp.float32)
    new_weight = (weight.astype(jnp.float32) - learn_rate * delta).astype(jnp.bfloat16)
    next_out = jnp.dot(next_acts, new_weight, preferred_element_type=jnp.float32).astype(jnp.bfloat16)
    return (next_out, new_weight, update)
```

```python
import jax
import jax.numpy as jnp
from jax import lax
from jax.experimental import pallas as pl
from jax.experimental.pallas import tpu as pltpu
from jax.sharding import Mesh
from jax.sharding import PartitionSpec as P

learn_rate = 0.02
beta_one = 0.9
beta_two = 0.999
epsilon = 1e-08
correct_first = 0.9999734386011124
correct_second = 0.0952078528862904

bf16 = jnp.bfloat16
f32 = jnp.float32


PLANE = ("y", "x")
FIRST_TOKENS = 96


def shift(value, axis, step=1):
    size = lax.axis_size(axis)
    return lax.ppermute(value, axis, [(i, (i + step) % size) for i in range(size)])


def swap(value, axes):
    return lax.all_to_all(value, axes, 0, 0, tiled=True)


def gather(block, axes):
    size = lax.axis_size(axes)
    return swap(jnp.broadcast_to(block[None], (size, *block.shape)), axes)


def around(block, axis):
    left = shift(block, axis, 1)
    right = shift(block, axis, -1)
    far = shift(block, axis, 2)
    return [block, left, far, right]


def plane_shift(value, outer, step):
    pairs = []
    for k in range(2):
        for y in range(4):
            for x in range(4):
                to_y, to_x = ((y + step) % 4, x) if (k == 0) == outer else (y, (x + step) % 4)
                pairs.append(((k * 4 + y) * 4 + x, (k * 4 + to_y) * 4 + to_x))
    return lax.ppermute(value, ("k", "y", "x"), pairs)


def plane_around(block, outer):
    left = plane_shift(block, outer, 1)
    right = plane_shift(block, outer, -1)
    far = plane_shift(block, outer, 2)
    return [block, left, far, right]


def decode(codes, exps):
    scale = jnp.exp2(exps.astype(f32))
    rows = codes.shape[0]
    values = (codes.astype(f32) / 128.0).reshape(rows, exps.shape[1], codes.shape[1] // exps.shape[1])
    return (values * scale[:, :, None]).reshape(rows, codes.shape[1])


def pair_order(mine, other, me):
    return jnp.where(me == 0, jnp.concatenate([mine, other], 0), jnp.concatenate([other, mine], 0))


def mm(a, b):
    return jnp.dot(a, b, preferred_element_type=f32)


def side_kernel(last, place, *refs):
    pieces, xs, proj = refs[:4], (refs[4:12], refs[12:20]), refs[20]
    if last:
        acc_in, low_in, direction, out = refs[21:25]
    else:
        acc, low = refs[21:23]
    w, xb, pb, wsem, xsem, psem = refs[-6:]
    rows, _ = pieces[0].shape[1:]
    feat = xb.shape[1] // 4
    side_h, k, z, y, x = (place[i] for i in range(5))

    def w_copy(src, to_y, to_x):
        at = pl.ds(pl.multiple_of(to_y * feat + to_x * rows, 32), rows)
        return pltpu.make_async_copy(src, w.at[at], wsem.at[to_y, to_x])

    def x_copy(src, chunk, n):
        at = pl.ds(0, FIRST_TOKENS) if n == 0 else pl.ds(FIRST_TOKENS, src.shape[0])
        to = pl.ds(pl.multiple_of(chunk * feat, 128), feat)
        return pltpu.make_async_copy(src, xb.at[at, to], xsem.at[chunk, n])

    def p_copy(i):
        return pltpu.make_async_copy(proj.at[4 * side_h + i], pb.at[pl.ds(i * feat, feat)], psem.at[i])

    for s in range(4):
        from_z = lax.rem(z - s + 4, 4)

        @pl.when(from_z // 2 == side_h)
        def _():
            for n in range(2):
                x_copy(xs[n][s], 2 * lax.rem(from_z, 2) + k, n).start()
                x_copy(xs[n][4 + s], 2 * lax.rem(from_z, 2) + 1 - k, n).start()

    for i in range(4):
        p_copy(i).start()
    for s in range(4):
        for t in range(4):
            back_y = jnp.where(k == 0, s, t)
            back_x = jnp.where(k == 0, t, s)
            w_copy(pieces[s].at[t], lax.rem(y - back_y + 4, 4), lax.rem(x - back_x + 4, 4)).start()
    for i in range(2):
        for j in (2 * i, 2 * i + 1):
            for n in range(2):
                x_copy(xs[n][0], j, n).wait()
            p_copy(j).wait()
            for t in range(4):
                w_copy(pieces[0].at[0], j, t).wait()
        at = slice(2 * i * feat, 2 * (i + 1) * feat)
        feats = xb[:, at]
        a = mm(feats, w[at])
        b = mm(feats, pb[at])
        if i == 0:
            total, total_low = (acc_in[...] + a, low_in[...] + b) if last else (a, b)
        else:
            total, total_low = total + a, total_low + b
    if last:
        out[...] = (total - learn_rate * mm(total_low.astype(bf16), direction[...])).astype(bf16)
    else:
        acc[...] = total
        low[...] = total_low


def side(place, pieces, xs, proj, *rest):
    _, _, width = pieces[0].shape
    feat = xs[0].shape[1]
    tok = xs[0].shape[0] + xs[8].shape[0]
    rank = proj.shape[-1]
    last = len(rest) > 0
    vmem = pl.BlockSpec(memory_space=pltpu.VMEM)
    hbm = pl.BlockSpec(memory_space=pl.ANY)
    if last:
        outs = jax.ShapeDtypeStruct((tok, width), bf16)
        out_specs = vmem
    else:
        outs = [jax.ShapeDtypeStruct((tok, width), f32), jax.ShapeDtypeStruct((tok, rank), f32)]
        out_specs = [vmem, vmem]
    return pl.pallas_call(
        lambda *refs: side_kernel(last, *refs),
        in_specs=[pl.BlockSpec(memory_space=pltpu.SMEM), *[hbm] * 21, *[vmem] * len(rest)],
        out_specs=out_specs,
        out_shape=outs,
        scratch_shapes=[
            pltpu.VMEM((4 * feat, width), bf16),
            pltpu.VMEM((tok, 4 * feat), bf16),
            pltpu.VMEM((4 * feat, rank), bf16),
            pltpu.SemaphoreType.DMA((4, 4)),
            pltpu.SemaphoreType.DMA((4, 2)),
            pltpu.SemaphoreType.DMA((4,)),
        ],
        compiler_params=pltpu.CompilerParams(vmem_limit_bytes=32 << 20),
        name="last_product" if last else "first_product",
    )(place, *pieces, *xs, proj, *rest)


def body(acts, out_grad, projection, weight, m_codes, m_exps, v_codes, v_exps, next_acts):
    k = lax.axis_index("k")
    z = lax.axis_index("z")
    h = lax.axis_index("h")
    tok, feat = acts.shape
    half = tok // 2
    rank = projection.shape[1]
    rows, width = weight.shape
    tokens_all = tok * lax.axis_size(("h", "y", "x"))

    mine = lax.dynamic_slice_in_dim(acts, k * half, half, 0)
    theirs = lax.dynamic_slice_in_dim(acts, (1 - k) * half, half, 0)
    got = shift(theirs, "k")
    p_mine = lax.dynamic_slice_in_dim(projection, (2 * z + k) * feat, feat, 0)
    p_got = lax.dynamic_slice_in_dim(projection, (2 * z + 1 - k) * feat, feat, 0)
    part = mm(mine, p_mine) + mm(got, p_got)
    low = swap(part.reshape(4, half // 4, rank), "z").sum(axis=0).astype(bf16)
    low = gather(low, "z").reshape(half, rank)
    lowrank = pair_order(low, shift(low, "k"), k)

    grad_part = lax.dot_general(lowrank, out_grad, (((0,), (0,)), ((), ())), preferred_element_type=f32)
    q = lax.axis_size(PLANE)
    own = rank // q // 2
    cut = grad_part.astype(bf16).reshape(2, q, own, width).transpose(1, 0, 2, 3).reshape(q, 2 * own, width)
    plane = swap(cut, PLANE).astype(f32).sum(axis=0)
    grad = (plane + shift(plane, "h")) / tokens_all

    moments = jnp.concatenate([decode(m_codes, m_exps), decode(v_codes, v_exps)], 0)
    other = shift(jnp.concatenate([weight, moments.astype(bf16)], 0), "h")
    shard = (weight, other[:rows])
    other = other[rows:].astype(f32)
    m_old = pair_order(moments[:own], other[:own], h)
    v_old = pair_order(moments[own:], other[own:], h)
    first = beta_one * m_old + (1.0 - beta_one) * grad
    second = beta_two * v_old + (1.0 - beta_two) * grad * grad
    both = first / correct_first / (jnp.sqrt(second / correct_second) + epsilon)
    update = jnp.where(h == 0, both[:own], both[own:])
    direction = gather(both.astype(bf16), PLANE)
    direction = direction.reshape(q, 2, own, width).transpose(1, 0, 2, 3).reshape(rank, width)

    xs = []
    for part in (next_acts[:FIRST_TOKENS], next_acts[FIRST_TOKENS:]):
        ring = around(part, "z")
        xs += ring
        xs += [shift(piece, "k") for piece in ring]

    proj = projection.reshape(8, feat, rank)
    rest = ()
    for s in (0, 1):
        block = jnp.stack(plane_around(shard[s], False))
        full = plane_around(block, True)
        place = jnp.stack([jnp.where(h == s, 0, 1), k, z, lax.axis_index("y"), lax.axis_index("x")]).astype(jnp.int32)
        rest = side(place, full, xs, proj, *rest)
        if s == 0:
            rest = (*rest, direction)
    out = rest

    p_rows = lax.dynamic_slice_in_dim(projection, lax.axis_index(("h", "y", "x")) * rows, rows, 0)
    new_weight = (weight.astype(f32) - learn_rate * mm(p_rows, direction)).astype(bf16)
    return (out, new_weight, update)


def solution(mesh):
    torus = Mesh(mesh.devices.reshape(mesh.shape["col"] // 2, 2, 2, 4, 4), ("z", "k", "h", "y", "x"))
    both = P(("h", "y", "x"), ("z", "k"))
    return jax.shard_map(
        body,
        mesh=torus,
        in_specs=(both, both, P(), both, both, both, both, both, both),
        out_specs=(both, both, both),
        check_vma=False,
    )
```

```python
import jax
import jax.numpy as jnp
from jax import lax
from jax.experimental import pallas as pl
from jax.experimental.pallas import tpu as pltpu
from jax.sharding import Mesh
from jax.sharding import PartitionSpec as P

learn_rate = 0.02
beta_one = 0.9
beta_two = 0.999
epsilon = 1e-08
correct_first = 0.9999734386011124
correct_second = 0.0952078528862904

bf16 = jnp.bfloat16
f32 = jnp.float32


PLANE = ("y", "x")


def shift(value, axis, step=1):
    size = lax.axis_size(axis)
    return lax.ppermute(value, axis, [(i, (i + step) % size) for i in range(size)])


def swap(value, axes):
    return lax.all_to_all(value, axes, 0, 0, tiled=True)


def gather(block, axes):
    size = lax.axis_size(axes)
    return swap(jnp.broadcast_to(block[None], (size, *block.shape)), axes)


def around(block, axis):
    left = shift(block, axis, 1)
    right = shift(block, axis, -1)
    far = shift(block, axis, 2)
    return [block, left, far, right]


def plane_shift(value, outer, step):
    pairs = []
    for k in range(2):
        for y in range(4):
            for x in range(4):
                to_y, to_x = ((y + step) % 4, x) if (k == 0) == outer else (y, (x + step) % 4)
                pairs.append(((k * 4 + y) * 4 + x, (k * 4 + to_y) * 4 + to_x))
    return lax.ppermute(value, ("k", "y", "x"), pairs)


def plane_around(block, outer):
    left = plane_shift(block, outer, 1)
    right = plane_shift(block, outer, -1)
    far = plane_shift(block, outer, 2)
    return [block, left, far, right]


def decode(m_codes, m_exps, v_codes, v_exps):
    scale = jnp.exp2(jnp.concatenate([m_exps, v_exps], 0).astype(f32)).astype(bf16)
    codes = jnp.concatenate([m_codes, v_codes], 0).astype(f32) / 128.0
    blocks, width = scale.shape[1], codes.shape[1]
    block_of = lax.broadcasted_iota(jnp.int32, (blocks, width), 1) // (width // blocks)
    ones = (block_of == lax.broadcasted_iota(jnp.int32, (blocks, width), 0)).astype(bf16)
    return codes * mm(scale, ones)


def pair_order(mine, other, me):
    return jnp.where(me == 0, jnp.concatenate([mine, other], 0), jnp.concatenate([other, mine], 0))


def mm(a, b):
    return jnp.dot(a, b, preferred_element_type=f32)


VMEM = pl.BlockSpec(memory_space=pltpu.VMEM)
SMEM = pl.BlockSpec(memory_space=pltpu.SMEM)
HBM = pl.BlockSpec(memory_space=pltpu.HBM)


def in_hbm(values):
    return [pltpu.with_memory_space_constraint(v, pltpu.HBM) for v in values]


def ranks_as_sent(rank, own):
    take = lax.broadcasted_iota(jnp.int32, (rank, rank), 0)
    col = lax.broadcasted_iota(jnp.int32, (rank, rank), 1)
    q = lax.div(col, 2 * own)
    half = lax.rem(lax.div(col, own), 2)
    return (take == half * (rank // 2) + q * own + lax.rem(col, own)).astype(bf16)


def first_kernel(place, *refs):
    pieces, xs, proj = refs[:4], refs[4:12], refs[12]
    acc, low, xt, w, xb, pb, wsem, xsem, psem = refs[13:]
    rows = pieces[0].shape[1]
    feat = xt.shape[2]
    h, k, z, y, x = (place[i] for i in range(5))

    def w_copy(src, to_y, to_x):
        at = pl.ds(pl.multiple_of(to_y * feat + to_x * rows, 32), rows)
        return pltpu.make_async_copy(src, w.at[at], wsem.at[to_y, to_x])

    def x_copy(src, side, chunk):
        to = pl.ds(pl.multiple_of(chunk * feat, 128), feat)
        return pltpu.make_async_copy(src, xb.at[side, :, to], xsem.at[side, chunk])

    def p_copy(side):
        half_h = jnp.where(side == 0, h, 1 - h)
        return pltpu.make_async_copy(proj.at[half_h], pb.at[side], psem.at[side])

    for s in range(4):
        from_z = lax.rem(z - s + 4, 4)
        side = jnp.where(from_z // 2 == h, 0, 1)
        x_copy(xs[s], side, 2 * lax.rem(from_z, 2) + k).start()
        x_copy(xs[4 + s], side, 2 * lax.rem(from_z, 2) + 1 - k).start()
    for s in range(4):
        for t in range(4):
            back_y = jnp.where(k == 0, s, t)
            back_x = jnp.where(k == 0, t, s)
            w_copy(pieces[s].at[t], lax.rem(y - back_y + 4, 4), lax.rem(x - back_x + 4, 4)).start()
    for i in range(2):
        p_copy(i).start()

    for i in range(2):
        for j in range(4):
            x_copy(xs[0], i, j).wait()

    @pl.when(k == 0)
    def _():
        for c in range(4):
            xt[c] = xb[1, :, c * feat : (c + 1) * feat]

    @pl.when(k == 1)
    def _():
        for c in range(4):
            xt[c] = jnp.concatenate(
                [xb[1, :, j * feat + c * rows : j * feat + (c + 1) * rows] for j in range(4)], axis=1
            )

    for i in range(2):
        for j in (2 * i, 2 * i + 1):
            for t in range(4):
                w_copy(pieces[0].at[0], j, t).wait()
        at = slice(2 * i * feat, 2 * (i + 1) * feat)
        part = mm(xb[0, :, at], w[at])
        total = part if i == 0 else total + part
    acc[...] = total
    for i in range(2):
        p_copy(i).wait()
    total_low = (mm(xb[0], pb[0]) + mm(xb[1], pb[1])).astype(bf16)
    low[...] = mm(total_low, ranks_as_sent(total_low.shape[1], 8)).astype(bf16)


def first_side(place, pieces, xs, proj):
    _, _, width = pieces[0].shape
    tok, feat = xs[0].shape
    rank = proj.shape[-1]
    shapes = [((tok, width), f32), ((tok, rank), bf16), ((4, tok, feat), bf16)]
    return pl.pallas_call(
        first_kernel,
        in_specs=[SMEM, *[HBM] * 13],
        out_specs=[VMEM] * 3,
        out_shape=[jax.ShapeDtypeStruct(*s) for s in shapes],
        scratch_shapes=[
            pltpu.VMEM((4 * feat, width), bf16),
            pltpu.VMEM((2, tok, 4 * feat), bf16),
            pltpu.VMEM((2, 4 * feat, rank), bf16),
            pltpu.SemaphoreType.DMA((4, 4)),
            pltpu.SemaphoreType.DMA((2, 4)),
            pltpu.SemaphoreType.DMA((2,)),
        ],
        compiler_params=pltpu.CompilerParams(vmem_limit_bytes=32 << 20),
        name="first_product",
    )(place, *in_hbm([*pieces, *xs, proj]))


def add_pieces(place, pieces, steps, xt, w, sem, total):
    rows = pieces[0].shape[1]
    k, y, x = (place[i] for i in (1, 3, 4))
    outer = jnp.where(k == 0, y, x)
    inner = jnp.where(k == 0, x, y)

    def w_copy(src, n, to):
        at = pl.ds(pl.multiple_of(to * rows, 32), rows)
        return pltpu.make_async_copy(src, w.at[n, at], sem.at[n, to])

    for n, piece in enumerate(pieces):
        for t in range(4):
            w_copy(piece.at[t], n, lax.rem(inner - t + 4, 4)).start()
    total = total()
    for n, (piece, s) in enumerate(zip(pieces, steps)):
        for t in range(4):
            w_copy(piece.at[0], n, t).wait()
        total = total + mm(xt[lax.rem(outer - s + 4, 4)], w[n])
    return total


def middle_kernel(place, a, b, c, xt, acc, out, w, sem):
    out[...] = add_pieces(place, (a, b, c), (0, 1, 3), xt, w, sem, lambda: acc[...])


def middle_side(place, pieces, xt, acc):
    count, rows, width = pieces[0].shape
    return pl.pallas_call(
        middle_kernel,
        in_specs=[SMEM, *[HBM] * 3, VMEM, VMEM],
        out_specs=VMEM,
        out_shape=jax.ShapeDtypeStruct(acc.shape, f32),
        scratch_shapes=[pltpu.VMEM((3, count * rows, width), bf16), pltpu.SemaphoreType.DMA((3, 4))],
        compiler_params=pltpu.CompilerParams(vmem_limit_bytes=32 << 20),
        name="middle_product",
    )(place, *in_hbm(pieces), xt, acc)


def last_kernel(place, far, proj, xt, acc, low, direction, weight, out, new_weight, w, pb, sem, psem):
    rows, width = weight.shape
    rank = low.shape[1]
    at = pl.ds(pl.multiple_of(place[5] * rows, 32), rows)
    p_copy = pltpu.make_async_copy(proj.at[at], pb, psem)
    p_copy.start()
    turned = direction[...].reshape(rank, width)

    def start():
        p_copy.wait()
        p_rows = mm(pb[...], ranks_as_sent(rank, 8)).astype(bf16)
        new_weight[...] = (weight[...].astype(f32) - learn_rate * mm(p_rows, turned)).astype(bf16)
        return acc[...] - learn_rate * mm(low[...], turned)

    out[...] = add_pieces(place, (far,), (2,), xt, w, sem, start).astype(bf16)


def last_side(place, far, proj, xt, acc, low, direction, weight):
    count, rows, width = far.shape
    return pl.pallas_call(
        last_kernel,
        in_specs=[SMEM, HBM, HBM, *[VMEM] * 5],
        out_specs=[VMEM, VMEM],
        out_shape=[jax.ShapeDtypeStruct(acc.shape, bf16), jax.ShapeDtypeStruct(weight.shape, bf16)],
        scratch_shapes=[
            pltpu.VMEM((1, count * rows, width), bf16),
            pltpu.VMEM((rows, proj.shape[1]), bf16),
            pltpu.SemaphoreType.DMA((1, 4)),
            pltpu.SemaphoreType.DMA,
        ],
        compiler_params=pltpu.CompilerParams(vmem_limit_bytes=32 << 20),
        name="last_product",
    )(place, *in_hbm([far, proj]), xt, acc, low, direction, weight)


def body(acts, out_grad, projection, weight, m_codes, m_exps, v_codes, v_exps, next_acts):
    k = lax.axis_index("k")
    z = lax.axis_index("z")
    h = lax.axis_index("h")
    tok, feat = acts.shape
    half = tok // 2
    rank = projection.shape[1]
    _, width = weight.shape
    tokens_all = tok * lax.axis_size(("h", "y", "x"))

    mine = lax.dynamic_slice_in_dim(acts, k * half, half, 0)
    theirs = lax.dynamic_slice_in_dim(acts, (1 - k) * half, half, 0)
    got = shift(theirs, "k")
    p_mine = lax.dynamic_slice_in_dim(projection, (2 * z + k) * feat, feat, 0)
    p_got = lax.dynamic_slice_in_dim(projection, (2 * z + 1 - k) * feat, feat, 0)
    part = mm(mine, p_mine) + mm(got, p_got)
    low = swap(part.reshape(4, half // 4, rank), "z").sum(axis=0).astype(bf16)
    low = gather(low, "z").reshape(half, rank)
    lowrank = pair_order(low, shift(low, "k"), k)

    grad_part = lax.dot_general(lowrank, out_grad, (((0,), (0,)), ((), ())), preferred_element_type=f32)
    q = lax.axis_size(PLANE)
    own = rank // q // 2
    cut = grad_part.astype(bf16).reshape(2, q, own, width).transpose(1, 0, 2, 3).reshape(q, 2 * own, width)
    plane = swap(cut, PLANE).astype(f32).sum(axis=0)
    moments = decode(m_codes, m_exps, v_codes, v_exps)
    other = shift(jnp.concatenate([plane, moments], 0), "h")
    grad = (plane + other[: 2 * own]) / tokens_all
    other = other[2 * own :]
    shard = (weight, shift(weight, "h"))
    m_old = pair_order(moments[:own], other[:own], h)
    v_old = pair_order(moments[own:], other[own:], h)
    first = beta_one * m_old + (1.0 - beta_one) * grad
    second = beta_two * v_old + (1.0 - beta_two) * grad * grad
    both = first / correct_first / (jnp.sqrt(second / correct_second) + epsilon)
    update = jnp.where(h == 0, both[:own], both[own:])
    direction = gather(both.astype(bf16), PLANE)

    xs = around(next_acts, "z")
    xs = [*xs, *(shift(piece, "k") for piece in xs)]

    sides = []
    for s in (0, 1):
        block = plane_around(shard[s], False)
        block = jnp.stack(block)
        sides.append(plane_around(block, True))
    place = [h, k, z, lax.axis_index("y"), lax.axis_index("x"), lax.axis_index(("h", "y", "x"))]
    place = jnp.stack(place).astype(jnp.int32)
    acc, next_low, xt = first_side(place, sides[0], xs, projection.reshape(2, 4 * feat, rank))
    mine_w, left, far, right = sides[1]
    acc = middle_side(place, [mine_w, left, right], xt, acc)
    out, new_weight = last_side(place, far, projection, xt, acc, next_low, direction, weight)
    return (out, new_weight, update)


def solution(mesh):
    torus = Mesh(mesh.devices.reshape(mesh.shape["col"] // 2, 2, 2, 4, 4), ("z", "k", "h", "y", "x"))
    both = P(("h", "y", "x"), ("z", "k"))
    return jax.shard_map(
        body,
        mesh=torus,
        in_specs=(both, both, P(), both, both, both, both, both, both),
        out_specs=(both, both, both),
        check_vma=False,
    )
```
